128 devices in a mesh: comp: 2 (over core), rank: 64 (over y, x, z).
Axes of the slice: x: 4, y: 4, z: 4, core: 2. Of those that a mesh axis runs over, the one named last changes fastest.
Arguments:
- surface_fields: bfloat16 [2, 40, 262144], P('comp', None, 'rank'), may hold values from -6 to 6
- cell_area: float32 [2, 262144], P('comp', 'rank'), may hold values from 0.5 to 2
- remap_tiles: bfloat16 [32768, 128, 128], P('rank'), may hold values from -0.5 to 0.5
- pair_blocks: int32 [64, 64], P('rank'), may hold values from 0 to 8, as said below
- slot_cell: int32 [64, 64, 8], P('rank'), may hold values from 0 to 31
- node_block: int32 [64, 512], P('rank'), may hold values from 0 to 31
Outputs:
- surface_fluxes: float32 [2, 20, 262144], P('comp', None, 'rank')
The draws below stay inside these ranges and needn't reach their ends.
Inputs may be any that keep to these rules, and one draw needn't show every extreme that they name: `pair_blocks`: entry [q, d] counts the live slots from atmosphere rank q to ocean rank d; in some rank's row every entry is 8.
All inputs are finite; a program needn't handle non-finite values.
Results may differ from the reference program's by a relative error of at most 0.0036.
Values may be sent and summed in bfloat16 or wider, within the bound.
A program may use at most 128 MiB of HBM per device.

```python
import math
import jax
import jax.numpy as jnp
from jax import lax

F_A = 40
F_F = 20
BS = 128
FLUX_IT = 5
NCB = 32
SLOTS = 8
NB = 512
NODES = 262144
N_RANK = 64


def draw_pair_blocks(key, part):
    key_level, key_busy, key_place = jax.random.split(key, 3)
    level = jax.random.randint(key_level, (N_RANK,), 0, 4)
    busiest = jax.random.randint(key_busy, (), 0, N_RANK)
    level = jnp.where(jnp.arange(N_RANK) == busiest, 3, level)
    factor = jnp.array([1, 2, 4, 8], jnp.int32)[level]
    live_total = SLOTS * N_RANK // 8 * factor
    position = jax.vmap(lambda subkey: jax.random.permutation(subkey, N_RANK))(jax.random.split(key_place, N_RANK))
    counts = (live_total[:, None] - position + N_RANK - 1) // N_RANK
    return jnp.clip(counts, 0, SLOTS).astype(jnp.int32)


def set_ends(values, stream_key, least, largest):
    longest = values.shape.index(max(values.shape))
    spots = []
    for shift in (0, 1):
        where = [jax.random.randint(jax.random.fold_in(stream_key, axis), (), 0, length) for axis, length in enumerate(values.shape)]
        where[longest] = (where[longest] + shift) % values.shape[longest]
        spots.append(tuple(where))
    return values.at[spots[0]].set(least).at[spots[1]].set(largest)


def block_levels(own_key, extent, cuts, low, largest):
    def one(dim, blocks):
        draws = jax.random.uniform(jax.random.fold_in(jax.random.fold_in(own_key, 6), dim), (blocks,), jnp.float32, low / len(cuts), largest / len(cuts))
        return jnp.repeat(jnp.exp(draws), extent[dim] // blocks).reshape((-1,) + (1,) * (len(extent) - dim - 1))

    level = one(*cuts[0])
    for cut in cuts[1:]:
        level = level * one(*cut)
    return level


def gaussian(own_key, dims, scale, most, cuts=(), held_as=jnp.bfloat16):
    gain = block_levels(own_key, dims, cuts, -0.22, 0.18) if cuts else 1.0
    entries = jax.random.normal(own_key, dims, jnp.float32) * scale * gain
    return jnp.minimum(jnp.maximum(entries, -most), most).astype(held_as)


def setup_inputs(seed: int = 0) -> dict:
    streams_of = jax.random.split(jax.random.key(seed), 7)
    surface_fields = gaussian(streams_of[0], (2, F_A, NODES), 1.0, 6.0, ((0, 2), (2, 64)))
    cell_area = jnp.clip(jnp.exp(math.log(2.0) - 1.3862944 * jax.random.uniform(streams_of[1], (2, NODES), jnp.float32) ** block_levels(streams_of[1], (2, NODES), ((0, 2), (1, 64)), -0.2, 0.2)), 0.5, 2.0)
    remap_tiles = gaussian(streams_of[2], (N_RANK * NB, BS, BS), BS ** -0.5, 0.5, ((0, 64),))
    pair_blocks = draw_pair_blocks(jax.random.fold_in(streams_of[6], 71), 0)
    slot_cell = set_ends(jax.random.randint(streams_of[4], (N_RANK, N_RANK, SLOTS), 0, NCB), jax.random.fold_in(streams_of[4], 1), 0, NCB - 1).astype(jnp.int32)
    node_block = set_ends(jax.random.randint(streams_of[5], (N_RANK, NB), 0, NCB), jax.random.fold_in(streams_of[5], 1), 0, NCB - 1).astype(jnp.int32)
    return dict(surface_fields=surface_fields, cell_area=cell_area, remap_tiles=remap_tiles, pair_blocks=pair_blocks, slot_cell=slot_cell, node_block=node_block)


def reference(surface_fields, cell_area, remap_tiles, pair_blocks, slot_cell, node_block):
    slot_total = SLOTS * N_RANK
    atmosphere = surface_fields[0].reshape(F_A, N_RANK, NCB, BS)
    ocean = surface_fields[1].astype(jnp.float32).reshape(F_A, N_RANK, NCB, BS).transpose(1, 2, 0, 3)
    tile_grid = remap_tiles.reshape(N_RANK, slot_total, BS, BS)
    live_mask = (jnp.arange(SLOTS)[None, None, :] < pair_blocks[:, :, None]).astype(jnp.float32).reshape(N_RANK, slot_total)
    dest_rank = jnp.repeat(jnp.arange(N_RANK, dtype=jnp.int32), SLOTS)
    slot_index = jnp.tile(jnp.arange(SLOTS, dtype=jnp.int32), N_RANK)

    def forward(carry, source_rank):
        blocks = jnp.take(atmosphere[:, source_rank], node_block[source_rank], axis=1)
        contrib = jnp.einsum('fjn,jnc->jfc', blocks.astype(jnp.float32), tile_grid[source_rank].astype(jnp.float32))
        contrib = contrib * live_mask[source_rank][:, None, None]
        contrib = lax.optimization_barrier(contrib.astype(jnp.bfloat16)).astype(jnp.float32)
        cell_index = slot_cell[dest_rank, source_rank, slot_index]
        return (carry.at[dest_rank, cell_index].add(contrib), None)
    start = jnp.zeros((N_RANK, NCB, F_A, BS), jnp.float32)
    remapped = lax.scan(forward, start, jnp.arange(N_RANK, dtype=jnp.int32))[0]
    wind_u = remapped[:, :, 0] - ocean[:, :, 0]
    wind_v = remapped[:, :, 1] - ocean[:, :, 1]
    wind_speed = jnp.sqrt(wind_u * wind_u + wind_v * wind_v + 0.25)
    stability = 1.0 + 4.0 * jax.nn.sigmoid(remapped[:, :, 2] - ocean[:, :, 2])
    transfer = jnp.ones_like(wind_speed)
    for sweep in range(FLUX_IT):
        transfer = 1.0 / (1.0 + stability * transfer)
    fluxes = (transfer * wind_speed)[:, :, None] * (remapped[:, :, :F_F] - ocean[:, :, :F_F]) + remapped[:, :, F_F:] * ocean[:, :, F_F:]
    weighted = (fluxes * cell_area[1].reshape(N_RANK, NCB, 1, BS)).astype(jnp.bfloat16)

    def backward(carry, source_rank):
        cell_index = slot_cell[dest_rank, source_rank, slot_index]
        pieces = weighted[dest_rank, cell_index]
        contrib = jnp.einsum('jfc,jnc->jfn', pieces.astype(jnp.float32), tile_grid[source_rank].astype(jnp.float32))
        contrib = contrib * live_mask[source_rank][:, None, None]
        node_sums = jnp.zeros((NCB, F_F, BS), jnp.float32).at[node_block[source_rank]].add(contrib)
        return (carry, node_sums)
    node_sums = lax.scan(backward, jnp.zeros((), jnp.float32), jnp.arange(N_RANK, dtype=jnp.int32))[1]
    atm_flux = node_sums.transpose(2, 0, 1, 3).reshape(F_F, NODES) / cell_area[0][None, :]
    ocean_flux = fluxes.transpose(2, 0, 1, 3).reshape(F_F, NODES)
    return jnp.stack([atm_flux, ocean_flux])
```

```python
import jax
import jax.numpy as jnp
from jax import lax
from jax.experimental import pallas as pl
from jax.experimental.pallas import tpu as pltpu
from jax.sharding import PartitionSpec as P

FLUX_IT = 5
MESH = pl.DeviceIdType.MESH
F32 = jnp.float32
BF16 = jnp.bfloat16

RANKS = 64
SLOTS = 8
NCB = 32
BS = 128
F_A = 40
F_F = 20
GROUPS = F_A // 8
CHUNK = 4
NCHUNK = RANKS // CHUNK
ROWS = SLOTS * 8
BACK_ROWS = SLOTS * F_F


def offset(k):
    return (k + k // 16) % 4, (k + k // 4) % 4, k % 4


def shifted(home, k, sign):
    dy, dx, dz = offset(k)
    y, x, z = home
    if sign < 0:
        dy, dx, dz = 4 - dy, 4 - dx, 4 - dz
    return ((y + dy) % 4) * 16 + ((x + dx) % 4) * 4 + (z + dz) % 4


def shifted_lanes(home, k, sign):
    y, x, z = home
    dy, dx, dz = (k + (k >> 4)) & 3, (k + (k >> 2)) & 3, k & 3
    if sign < 0:
        dy, dx, dz = 4 - dy, 4 - dx, 4 - dz
    return ((y + dy) & 3) * 16 + ((x + dx) & 3) * 4 + ((z + dz) & 3)


def kernel(
    fields, area, tiles, nblk, pair, cell, cell_v, nblk_v, pair_v,
    out,
    tvm, blk, sbuf, rbuf, bsbuf, brbuf, pick, pick2, acc, osurf, wind, wt, stage, stage2, sums2,
    tsem, ssem, rsem, bssem, brsem,
):
    comp = lax.axis_index("comp")
    rank = lax.axis_index("rank")
    home = (rank // 16, (rank // 4) % 4, rank % 4)

    def to_ocean(k):
        return pltpu.make_async_remote_copy(
            src_ref=sbuf.at[k], dst_ref=rbuf.at[k], send_sem=ssem.at[k], recv_sem=rsem.at[k],
            device_id=(1, shifted(home, k, 1)), device_id_type=MESH,
        )

    def to_atmosphere(k):
        return pltpu.make_async_remote_copy(
            src_ref=bsbuf.at[k], dst_ref=brbuf.at[k], send_sem=bssem.at[k], recv_sem=brsem.at[k],
            device_id=(0, shifted(home, k, -1)), device_id_type=MESH,
        )

    def load_tiles(k):
        return pltpu.make_async_copy(tiles.at[shifted(home, k, 1)], tvm.at[k], tsem.at[k])

    barrier = pltpu.get_barrier_semaphore()

    def greet(k, carry):
        pl.semaphore_signal(
            barrier, inc=1, device_id=(1 - comp, shifted(home, k, 1)), device_id_type=MESH
        )
        return carry

    def permuted(b):
        columns = pl.ds(pl.multiple_of(b * BS, BS), BS)
        x = fields[:, columns].astype(F32)
        return [
            x[0:8], x[8:16], jnp.concatenate([x[16:20], x[36:40]], axis=0), x[20:28], x[28:36],
        ]

    @pl.when(comp == 0)
    def _():
        def begin(k, carry):
            load_tiles(k).start()
            return carry

        lax.fori_loop(0, RANKS, begin, 0)
        lax.fori_loop(0, RANKS, greet, 0)

        def arrange(b, carry):
            blk[b] = jnp.concatenate(permuted(b), axis=0).astype(BF16)
            return carry

        lax.fori_loop(0, NCB, arrange, 0)

        def products(k):
            d = shifted(home, k, 1)
            load_tiles(k).wait()
            live = pair[0, d]
            for s in range(0, SLOTS, 2):
                both = []
                for e in (s, s + 1):
                    lhs = blk[nblk[0, d * SLOTS + e]]
                    r = jnp.dot(lhs, tvm[k, e], preferred_element_type=F32)
                    both.append(r * (e < live).astype(F32))
                for g in range(GROUPS):
                    rows = slice(g * 8, g * 8 + 8)
                    sbuf[k, g, s * 8 : s * 8 + 16, :] = jnp.concatenate(
                        [both[0][rows], both[1][rows]], axis=0
                    ).astype(BF16)

        AHEAD = 4
        for k in range(AHEAD):
            products(k)
        pl.semaphore_wait(barrier, RANKS)
        for k in range(AHEAD):
            to_ocean(k).start()

        def step(k, carry):
            products(k)
            to_ocean(k).start()
            return carry

        lax.fori_loop(AHEAD, RANKS, step, 0)

        def build(i, carry):
            lane = lax.broadcasted_iota(jnp.int32, (1, 256), 1)
            kk = i * CHUNK + (lane >> 6)
            where_k = shifted_lanes(home, kk, 1)
            slot = (lane >> 3) & 7
            q = lax.broadcasted_iota(jnp.int32, (RANKS, 256), 0)
            j = lax.broadcasted_iota(jnp.int32, (RANKS * SLOTS, 256), 0)
            ej = (j == where_k * SLOTS + slot).astype(F32).astype(BF16)
            ed = (q == where_k).astype(F32).astype(BF16)
            nb = jnp.broadcast_to(nblk_v[...].astype(F32), (8, RANKS * SLOTS)).astype(BF16)
            pb = jnp.broadcast_to(pair_v[...].astype(F32), (8, RANKS)).astype(BF16)
            block = jnp.dot(nb, ej, preferred_element_type=F32)[0:1]
            count = jnp.dot(pb, ed, preferred_element_type=F32)[0:1]
            block = jnp.where(slot.astype(F32) < count, block, 100.0)
            key = block * 8.0 + (lane & 7).astype(F32)
            row = lax.broadcasted_iota(jnp.int32, (256, 256), 0).astype(F32)
            pick[i] = (row == key).astype(F32).astype(BF16)
            lane = lax.broadcasted_iota(jnp.int32, (1, 128), 1)
            kk = i * CHUNK + (lane >> 5)
            where_k = shifted_lanes(home, kk, 1)
            slot = (lane >> 2) & 7
            q = lax.broadcasted_iota(jnp.int32, (RANKS, 128), 0)
            j = lax.broadcasted_iota(jnp.int32, (RANKS * SLOTS, 128), 0)
            ej = (j == where_k * SLOTS + slot).astype(F32).astype(BF16)
            ed = (q == where_k).astype(F32).astype(BF16)
            block = jnp.dot(nb, ej, preferred_element_type=F32)[0:1]
            count = jnp.dot(pb, ed, preferred_element_type=F32)[0:1]
            block = jnp.where(slot.astype(F32) < count, block, 100.0)
            key = block * 4.0 + (lane & 3).astype(F32)
            row = lax.broadcasted_iota(jnp.int32, (128, 128), 0).astype(F32)
            pick2[i] = (row == key).astype(F32).astype(BF16)
            return carry

        lax.fori_loop(0, NCHUNK, build, 0)
        acc[...] = jnp.zeros_like(acc)
        sums2[...] = jnp.zeros_like(sums2)

        def split(r):
            hi = r.astype(BF16)
            return jnp.concatenate([hi, (r - hi.astype(F32)).astype(BF16)], axis=1)

        def back(i, carry):
            for c in range(CHUNK):
                k = i * CHUNK + c
                to_atmosphere(k).wait_recv()
                for p in range(SLOTS // 2):
                    lhs = jnp.concatenate(
                        [
                            brbuf[k, p * 16 : p * 16 + 16],
                            brbuf[k, 64 + p * 16 : 64 + p * 16 + 16],
                            brbuf[k, 128 + p * 8 : 128 + p * 8 + 8],
                        ],
                        axis=0,
                    )
                    rhs = tvm[k, 2 * p : 2 * p + 2].reshape(2 * BS, BS)
                    r = lax.dot_general(
                        lhs, rhs, (((1,), (1,)), ((), ())), preferred_element_type=F32
                    )
                    low, high = r[:, :BS], r[:, BS:]
                    rows = slice(c * 64 + p * 16, c * 64 + p * 16 + 16)
                    stage[0, rows] = split(jnp.concatenate([low[0:8], high[8:16]], axis=0))
                    stage[1, rows] = split(jnp.concatenate([low[16:24], high[24:32]], axis=0))
                    sub = lax.broadcasted_iota(jnp.int32, (8, BS), 0)
                    last = jnp.where(sub < 4, low[32:40], high[32:40])
                    rows = slice(c * 32 + p * 8, c * 32 + p * 8 + 8)
                    stage2[rows] = split(last)
            for g in (0, 1):
                r = jnp.dot(pick[i], stage[g], preferred_element_type=F32)
                acc[g] += r[:, :BS] + r[:, BS:]
            r = jnp.dot(pick2[i], stage2[...], preferred_element_type=F32)
            sums2[...] += r[:, :BS] + r[:, BS:]
            return carry

        lax.fori_loop(0, NCHUNK, back, 0)

        for b in range(NCB):
            a = area[0:1, b * BS : (b + 1) * BS]
            out[0:8, b * BS : (b + 1) * BS] = acc[0, b * 8 : b * 8 + 8] / a
            out[8:16, b * BS : (b + 1) * BS] = acc[1, b * 8 : b * 8 + 8] / a
            out[16:20, b * BS : (b + 1) * BS] = sums2[b * 4 : b * 4 + 4] / a

        def sent(k, carry):
            to_ocean(k).wait_send()
            return carry

        lax.fori_loop(0, RANKS, sent, 0)

    @pl.when(comp == 1)
    def _():
        lax.fori_loop(0, RANKS, greet, 0)

        def arrange(b, carry):
            rows = pl.ds(pl.multiple_of(b * 8, 8), 8)
            for g, part in enumerate(permuted(b)):
                osurf[g, rows] = part
            return carry

        lax.fori_loop(0, NCB, arrange, 0)

        def build(i, carry):
            lane = lax.broadcasted_iota(jnp.int32, (1, 256), 1)
            kk = i * CHUNK + (lane >> 6)
            where_k = shifted_lanes(home, kk, -1)
            slot = (lane >> 3) & 7
            q = lax.broadcasted_iota(jnp.int32, (RANKS, 256), 0)
            ed = (q == where_k).astype(F32).astype(BF16)
            cells = jnp.dot(cell_v[...].astype(F32).astype(BF16), ed, preferred_element_type=F32)
            s = lax.broadcasted_iota(jnp.int32, (SLOTS, 256), 0)
            mine = jnp.sum(jnp.where(s == slot, cells, 0.0), axis=0, keepdims=True)
            key = mine * 8.0 + (lane & 7).astype(F32)
            row = lax.broadcasted_iota(jnp.int32, (256, 256), 0).astype(F32)
            pick[i] = (row == key).astype(F32).astype(BF16)
            return carry

        lax.fori_loop(0, NCHUNK, build, 0)
        acc[...] = jnp.zeros_like(acc)
        pl.semaphore_wait(barrier, RANKS)

        def reduce(i, carry):
            for c in range(CHUNK):
                to_ocean(i * CHUNK + c).wait_recv()
            for g in range(GROUPS):
                rhs = rbuf[pl.ds(i * CHUNK, CHUNK), g].reshape(CHUNK * ROWS, BS)
                acc[g] += jnp.dot(pick[i], rhs, preferred_element_type=F32)
            return carry

        lax.fori_loop(0, NCHUNK, reduce, 0)

        def difference(f):
            rows = pl.ds(f, NCB, stride=8)
            return acc[0, rows, :] - osurf[0, rows, :]

        wind_u = difference(0)
        wind_v = difference(1)
        wind_speed = jnp.sqrt(wind_u * wind_u + wind_v * wind_v + 0.25)
        stability = 1.0 + 4.0 * jax.nn.sigmoid(difference(2))
        transfer = jnp.ones_like(wind_speed)
        for sweep in range(FLUX_IT):
            transfer = 1.0 / (1.0 + stability * transfer)
        wind[...] = transfer * wind_speed

        for c in range(NCB):
            rows = slice(c * 8, c * 8 + 8)
            columns = slice(c * BS, (c + 1) * BS)
            scale = jnp.broadcast_to(wind[c : c + 1], (8, BS))
            a = jnp.broadcast_to(area[0:1, columns], (8, BS))
            x = [acc[g, rows] for g in range(GROUPS)]
            o = [osurf[g, rows] for g in range(GROUPS)]
            first = scale * (x[0] - o[0]) + x[3] * o[3]
            second = scale * (x[1] - o[1]) + x[4] * o[4]
            third = scale * (x[2] - o[2]) + pltpu.roll(x[2] * o[2], 4, 0)
            out[0:8, columns] = first
            out[8:16, columns] = second
            out[16:20, columns] = third[0:4]
            sub = lax.broadcasted_iota(jnp.int32, (8, BS), 0)
            third = jnp.where(sub < 4, third * a, 0.0).astype(BF16).astype(F32)
            wt[c, 0] = (first * a).astype(BF16).astype(F32)
            wt[c, 1] = (second * a).astype(BF16).astype(F32)
            wt[c, 2] = third
            wt[c, 3] = pltpu.roll(third, 4, 0)

        def send_back(k, carry):
            q = shifted(home, k, -1)
            cells = [cell[s, q] for s in range(SLOTS)]
            for g in (0, 1):
                for s in range(0, SLOTS, 2):
                    bsbuf[k, g * 64 + s * 8 : g * 64 + s * 8 + 16] = jnp.concatenate(
                        [wt[cells[s], g], wt[cells[s + 1], g]], axis=0
                    ).astype(BF16)
            for s in range(0, SLOTS, 4):
                bsbuf[k, 128 + s * 4 : 128 + s * 4 + 16] = jnp.concatenate(
                    [
                        wt[cells[s], 2] + wt[cells[s + 1], 3],
                        wt[cells[s + 2], 2] + wt[cells[s + 3], 3],
                    ],
                    axis=0,
                ).astype(BF16)
            to_atmosphere(k).start()
            return carry

        lax.fori_loop(0, RANKS, send_back, 0)

        def sent(k, carry):
            to_atmosphere(k).wait_send()
            return carry

        lax.fori_loop(0, RANKS, sent, 0)


def on_device(surface_fields, cell_area, remap_tiles, pair_blocks, slot_cell, node_block):
    vmem = pl.BlockSpec(memory_space=pltpu.VMEM)
    smem = pl.BlockSpec(memory_space=pltpu.SMEM)
    cells = slot_cell[0].T
    out = pl.pallas_call(
        kernel,
        out_shape=jax.ShapeDtypeStruct((F_F, NCB * BS), F32),
        in_specs=[vmem, vmem, pl.BlockSpec(memory_space=pl.ANY), smem, smem, smem, vmem, vmem, vmem],
        out_specs=vmem,
        scratch_shapes=[
            pltpu.VMEM((RANKS, SLOTS, BS, BS), BF16),
            pltpu.VMEM((NCB, F_A, BS), BF16),
            pltpu.VMEM((RANKS, GROUPS, ROWS, BS), BF16),
            pltpu.VMEM((RANKS, GROUPS, ROWS, BS), BF16),
            pltpu.VMEM((RANKS, BACK_ROWS, BS), BF16),
            pltpu.VMEM((RANKS, BACK_ROWS, BS), BF16),
            pltpu.VMEM((NCHUNK, 256, 256), BF16),
            pltpu.VMEM((NCHUNK, 128, 128), BF16),
            pltpu.VMEM((GROUPS, NCB * 8, BS), F32),
            pltpu.VMEM((GROUPS, NCB * 8, BS), F32),
            pltpu.VMEM((NCB, BS), F32),
            pltpu.VMEM((NCB, 4, 8, BS), F32),
            pltpu.VMEM((2, 256, 2 * BS), BF16),
            pltpu.VMEM((128, 2 * BS), BF16),
            pltpu.VMEM((NCB * 4, BS), F32),
            pltpu.SemaphoreType.DMA((RANKS,)),
            pltpu.SemaphoreType.DMA((RANKS,)),
            pltpu.SemaphoreType.DMA((RANKS,)),
            pltpu.SemaphoreType.DMA((RANKS,)),
            pltpu.SemaphoreType.DMA((RANKS,)),
        ],
        compiler_params=pltpu.CompilerParams(
            collective_id=0, has_side_effects=True, vmem_limit_bytes=56 << 20
        ),
    )(
        surface_fields[0], cell_area, remap_tiles.reshape(RANKS, SLOTS, BS, BS),
        node_block, pair_blocks, cells, cells, node_block, pair_blocks,
    )
    return out[None]


def solution(mesh):
    return jax.shard_map(
        on_device,
        mesh=mesh,
        in_specs=(
            P("comp", None, "rank"),
            P("comp", "rank"),
            P("rank", None, None),
            P("rank", None),
            P("rank", None, None),
            P("rank", None),
        ),
        out_specs=P("comp", None, "rank"),
        check_vma=False,
    )
```

```python
import jax
import jax.numpy as jnp
from jax import lax
from jax.experimental import pallas as pl
from jax.experimental.pallas import tpu as pltpu
from jax.sharding import PartitionSpec as P

FLUX_IT = 5
MESH = pl.DeviceIdType.MESH
F32 = jnp.float32
BF16 = jnp.bfloat16

RANKS = 64
SLOTS = 8
NCB = 32
BS = 128
F_A = 40
F_F = 20
GROUPS = F_A // 8
CHUNK = 4
NCHUNK = RANKS // CHUNK
ROWS = SLOTS * 8
BACK_ROWS = SLOTS * F_F


def offset(k):
    return (k + (k >> 4)) & 3, (k + (k >> 2)) & 3, k & 3


def shifted(home, k, sign):
    dy, dx, dz = offset(k)
    y, x, z = home
    if sign < 0:
        dy, dx, dz = 4 - dy, 4 - dx, 4 - dz
    return (((y + dy) & 3) << 4) + (((x + dx) & 3) << 2) + ((z + dz) & 3)


def kernel(
    fields, area, tiles, nblk, pair, cell, cell_v, nblk_v, pair_v,
    out,
    tvm, blk, sbuf, rbuf, bsbuf, brbuf, pick, pick2, acc, osurf, wind, wt, stage, stage2, sums2,
    tsem, ssem, rsem, bssem, brsem,
):
    comp = lax.axis_index("comp")
    rank = lax.axis_index("rank")
    home = (rank >> 4, (rank >> 2) & 3, rank & 3)

    def to_ocean(k):
        return pltpu.make_async_remote_copy(
            src_ref=sbuf.at[k], dst_ref=rbuf.at[k], send_sem=ssem.at[k], recv_sem=rsem.at[k],
            device_id=(1, shifted(home, k, 1)), device_id_type=MESH,
        )

    def to_atmosphere(k):
        return pltpu.make_async_remote_copy(
            src_ref=bsbuf.at[k], dst_ref=brbuf.at[k], send_sem=bssem.at[k], recv_sem=brsem.at[k],
            device_id=(0, shifted(home, k, -1)), device_id_type=MESH,
        )

    def load_tiles(k):
        return pltpu.make_async_copy(tiles.at[shifted(home, k, 1)], tvm.at[k], tsem.at[k])

    barrier = pltpu.get_barrier_semaphore()

    def greet(k, carry):
        pl.semaphore_signal(
            barrier, inc=1, device_id=(1 - comp, (rank + k) & (RANKS - 1)), device_id_type=MESH
        )
        return carry

    lax.fori_loop(0, RANKS, greet, 0)

    def permuted(b):
        columns = pl.ds(pl.multiple_of(b * BS, BS), BS)
        x = fields[:, columns].astype(F32)
        return [
            x[0:8], x[8:16], jnp.concatenate([x[16:20], x[36:40]], axis=0), x[20:28], x[28:36],
        ]

    @pl.when(comp == 0)
    def _():
        def begin(k, carry):
            load_tiles(k).start()
            return carry

        lax.fori_loop(0, RANKS, begin, 0)

        def arrange(b, carry):
            blk[b] = jnp.concatenate(permuted(b), axis=0).astype(BF16)
            return carry

        lax.fori_loop(0, NCB, arrange, 0)

        def products(k):
            d = shifted(home, k, 1)
            load_tiles(k).wait()
            live = pair[0, d]
            for s in range(0, SLOTS, 2):
                both = []
                for e in (s, s + 1):
                    lhs = blk[nblk[0, d * SLOTS + e]]
                    r = jnp.dot(lhs, tvm[k, e], preferred_element_type=F32)
                    both.append(r * (e < live).astype(F32))
                for g in range(GROUPS):
                    rows = slice(g * 8, g * 8 + 8)
                    sbuf[k, g, s * 8 : s * 8 + 16, :] = jnp.concatenate(
                        [both[0][rows], both[1][rows]], axis=0
                    ).astype(BF16)

        AHEAD = 4
        def ahead(k, carry):
            products(k)
            return carry

        def release(k, carry):
            to_ocean(k).start()
            return carry

        def step(k, carry):
            products(k)
            to_ocean(k).start()
            return carry

        lax.fori_loop(0, AHEAD, ahead, 0)
        pl.semaphore_wait(barrier, RANKS)
        lax.fori_loop(0, AHEAD, release, 0)
        lax.fori_loop(AHEAD, RANKS, step, 0)

        def build(i, carry):
            lane = lax.broadcasted_iota(jnp.int32, (1, 256), 1)
            kk = i * CHUNK + (lane >> 6)
            where_k = shifted(home, kk, 1)
            slot = (lane >> 3) & 7
            q = lax.broadcasted_iota(jnp.int32, (RANKS, 256), 0)
            j = lax.broadcasted_iota(jnp.int32, (RANKS * SLOTS, 256), 0)
            ej = (j == where_k * SLOTS + slot).astype(F32).astype(BF16)
            ed = (q == where_k).astype(F32).astype(BF16)
            nb = jnp.broadcast_to(nblk_v[...].astype(F32), (8, RANKS * SLOTS)).astype(BF16)
            pb = jnp.broadcast_to(pair_v[...].astype(F32), (8, RANKS)).astype(BF16)
            block = jnp.dot(nb, ej, preferred_element_type=F32)[0:1]
            count = jnp.dot(pb, ed, preferred_element_type=F32)[0:1]
            block = jnp.where(slot.astype(F32) < count, block, 100.0)
            key = block * 8.0 + (lane & 7).astype(F32)
            row = lax.broadcasted_iota(jnp.int32, (256, 256), 0).astype(F32)
            pick[i] = (row == key).astype(F32).astype(BF16)
            lane = lax.broadcasted_iota(jnp.int32, (1, 128), 1)
            kk = i * CHUNK + (lane >> 5)
            where_k = shifted(home, kk, 1)
            slot = (lane >> 2) & 7
            q = lax.broadcasted_iota(jnp.int32, (RANKS, 128), 0)
            j = lax.broadcasted_iota(jnp.int32, (RANKS * SLOTS, 128), 0)
            ej = (j == where_k * SLOTS + slot).astype(F32).astype(BF16)
            ed = (q == where_k).astype(F32).astype(BF16)
            block = jnp.dot(nb, ej, preferred_element_type=F32)[0:1]
            count = jnp.dot(pb, ed, preferred_element_type=F32)[0:1]
            block = jnp.where(slot.astype(F32) < count, block, 100.0)
            key = block * 4.0 + (lane & 3).astype(F32)
            row = lax.broadcasted_iota(jnp.int32, (128, 128), 0).astype(F32)
            pick2[i] = (row == key).astype(F32).astype(BF16)
            return carry

        lax.fori_loop(0, NCHUNK, build, 0)
        acc[...] = jnp.zeros_like(acc)
        sums2[...] = jnp.zeros_like(sums2)

        def split(r):
            hi = r.astype(BF16)
            return jnp.concatenate([hi, (r - hi.astype(F32)).astype(BF16)], axis=1)

        def collect(i, half):
            for g in (0, 1):
                r = jnp.dot(pick[i], stage[half, g], preferred_element_type=F32)
                acc[g] += r[:, :BS] + r[:, BS:]
            r = jnp.dot(pick2[i], stage2[half], preferred_element_type=F32)
            sums2[...] += r[:, :BS] + r[:, BS:]

        def back_products(i, half):
            for c in range(CHUNK):
                k = i * CHUNK + c
                for p in range(SLOTS // 2):
                    lhs = jnp.concatenate(
                        [
                            brbuf[k, p * 16 : p * 16 + 16],
                            brbuf[k, 64 + p * 16 : 64 + p * 16 + 16],
                            brbuf[k, 128 + p * 8 : 128 + p * 8 + 8],
                        ],
                        axis=0,
                    )
                    rhs = tvm[k, 2 * p : 2 * p + 2].reshape(2 * BS, BS)
                    r = lax.dot_general(
                        lhs, rhs, (((1,), (1,)), ((), ())), preferred_element_type=F32
                    )
                    low, high = r[:, :BS], r[:, BS:]
                    rows = slice(c * 64 + p * 16, c * 64 + p * 16 + 16)
                    stage[half, 0, rows] = split(jnp.concatenate([low[0:8], high[8:16]], axis=0))
                    stage[half, 1, rows] = split(jnp.concatenate([low[16:24], high[24:32]], axis=0))
                    sub = lax.broadcasted_iota(jnp.int32, (8, BS), 0)
                    last = jnp.where(sub < 4, low[32:40], high[32:40])
                    rows = slice(c * 32 + p * 8, c * 32 + p * 8 + 8)
                    stage2[half, rows] = split(last)

        def arrived(i):
            for c in range(CHUNK):
                to_atmosphere(i * CHUNK + c).wait_recv()

        arrived(0)
        back_products(0, 0)

        def back(m, carry):
            for e in range(2):
                i = 2 * m + 1 + e
                arrived(i)
                collect(i - 1, e)
                back_products(i, 1 - e)
            return carry

        lax.fori_loop(0, (NCHUNK - 2) // 2, back, 0)
        arrived(NCHUNK - 1)
        collect(NCHUNK - 2, 0)
        back_products(NCHUNK - 1, 1)
        collect(NCHUNK - 1, 1)

        for b in range(NCB):
            a = area[0:1, b * BS : (b + 1) * BS]
            out[0:8, b * BS : (b + 1) * BS] = acc[0, b * 8 : b * 8 + 8] / a
            out[8:16, b * BS : (b + 1) * BS] = acc[1, b * 8 : b * 8 + 8] / a
            out[16:20, b * BS : (b + 1) * BS] = sums2[b * 4 : b * 4 + 4] / a

        def sent(k, carry):
            to_ocean(k).wait_send()
            return carry

        lax.fori_loop(0, RANKS, sent, 0)

    @pl.when(comp == 1)
    def _():
        def arrange(b, carry):
            rows = pl.ds(pl.multiple_of(b * 8, 8), 8)
            for g, part in enumerate(permuted(b)):
                osurf[g, rows] = part
            return carry

        lax.fori_loop(0, NCB, arrange, 0)

        def build(i, carry):
            lane = lax.broadcasted_iota(jnp.int32, (1, 256), 1)
            kk = i * CHUNK + (lane >> 6)
            where_k = shifted(home, kk, -1)
            slot = (lane >> 3) & 7
            q = lax.broadcasted_iota(jnp.int32, (RANKS, 256), 0)
            ed = (q == where_k).astype(F32).astype(BF16)
            cells = jnp.dot(cell_v[...].astype(F32).astype(BF16), ed, preferred_element_type=F32)
            s = lax.broadcasted_iota(jnp.int32, (SLOTS, 256), 0)
            mine = jnp.sum(jnp.where(s == slot, cells, 0.0), axis=0, keepdims=True)
            key = mine * 8.0 + (lane & 7).astype(F32)
            row = lax.broadcasted_iota(jnp.int32, (256, 256), 0).astype(F32)
            pick[i] = (row == key).astype(F32).astype(BF16)
            return carry

        lax.fori_loop(0, NCHUNK, build, 0)
        acc[...] = jnp.zeros_like(acc)
        pl.semaphore_wait(barrier, RANKS)

        def reduce(i, carry):
            for c in range(CHUNK):
                to_ocean(i * CHUNK + c).wait_recv()
            for g in range(GROUPS):
                rhs = rbuf[pl.ds(i * CHUNK, CHUNK), g].reshape(CHUNK * ROWS, BS)
                acc[g] += jnp.dot(pick[i], rhs, preferred_element_type=F32)
            return carry

        lax.fori_loop(0, NCHUNK, reduce, 0)

        def difference(f):
            rows = pl.ds(f, NCB, stride=8)
            return acc[0, rows, :] - osurf[0, rows, :]

        wind_u = difference(0)
        wind_v = difference(1)
        wind_speed = jnp.sqrt(wind_u * wind_u + wind_v * wind_v + 0.25)
        stability = 1.0 + 4.0 * jax.nn.sigmoid(difference(2))
        transfer = jnp.ones_like(wind_speed)
        for sweep in range(FLUX_IT):
            transfer = 1.0 / (1.0 + stability * transfer)
        wind[...] = transfer * wind_speed

        for c in range(NCB):
            rows = slice(c * 8, c * 8 + 8)
            columns = slice(c * BS, (c + 1) * BS)
            scale = jnp.broadcast_to(wind[c : c + 1], (8, BS))
            a = jnp.broadcast_to(area[0:1, columns], (8, BS))
            x = [acc[g, rows] for g in range(GROUPS)]
            o = [osurf[g, rows] for g in range(GROUPS)]
            first = scale * (x[0] - o[0]) + x[3] * o[3]
            second = scale * (x[1] - o[1]) + x[4] * o[4]
            third = scale * (x[2] - o[2]) + pltpu.roll(x[2] * o[2], 4, 0)
            out[0:8, columns] = first
            out[8:16, columns] = second
            out[16:20, columns] = third[0:4]
            sub = lax.broadcasted_iota(jnp.int32, (8, BS), 0)
            third = jnp.where(sub < 4, third * a, 0.0).astype(BF16).astype(F32)
            wt[c, 0] = (first * a).astype(BF16).astype(F32)
            wt[c, 1] = (second * a).astype(BF16).astype(F32)
            wt[c, 2] = third
            wt[c, 3] = pltpu.roll(third, 4, 0)

        def send_back(k, carry):
            q = shifted(home, k, -1)
            cells = [cell[s, q] for s in range(SLOTS)]
            for g in (0, 1):
                for s in range(0, SLOTS, 2):
                    bsbuf[k, g * 64 + s * 8 : g * 64 + s * 8 + 16] = jnp.concatenate(
                        [wt[cells[s], g], wt[cells[s + 1], g]], axis=0
                    ).astype(BF16)
            for s in range(0, SLOTS, 4):
                bsbuf[k, 128 + s * 4 : 128 + s * 4 + 16] = jnp.concatenate(
                    [
                        wt[cells[s], 2] + wt[cells[s + 1], 3],
                        wt[cells[s + 2], 2] + wt[cells[s + 3], 3],
                    ],
                    axis=0,
                ).astype(BF16)
            to_atmosphere(k).start()
            return carry

        lax.fori_loop(0, RANKS, send_back, 0)

        def sent(k, carry):
            to_atmosphere(k).wait_send()
            return carry

        lax.fori_loop(0, RANKS, sent, 0)


def on_device(surface_fields, cell_area, remap_tiles, pair_blocks, slot_cell, node_block):
    vmem = pl.BlockSpec(memory_space=pltpu.VMEM)
    smem = pl.BlockSpec(memory_space=pltpu.SMEM)
    cells = slot_cell[0].T
    out = pl.pallas_call(
        kernel,
        out_shape=jax.ShapeDtypeStruct((F_F, NCB * BS), F32),
        in_specs=[vmem, vmem, pl.BlockSpec(memory_space=pl.ANY), smem, smem, smem, vmem, vmem, vmem],
        out_specs=vmem,
        scratch_shapes=[
            pltpu.VMEM((RANKS, SLOTS, BS, BS), BF16),
            pltpu.VMEM((NCB, F_A, BS), BF16),
            pltpu.VMEM((RANKS, GROUPS, ROWS, BS), BF16),
            pltpu.VMEM((RANKS, GROUPS, ROWS, BS), BF16),
            pltpu.VMEM((RANKS, BACK_ROWS, BS), BF16),
            pltpu.VMEM((RANKS, BACK_ROWS, BS), BF16),
            pltpu.VMEM((NCHUNK, 256, 256), BF16),
            pltpu.VMEM((NCHUNK, 128, 128), BF16),
            pltpu.VMEM((GROUPS, NCB * 8, BS), F32),
            pltpu.VMEM((GROUPS, NCB * 8, BS), F32),
            pltpu.VMEM((NCB, BS), F32),
            pltpu.VMEM((NCB, 4, 8, BS), F32),
            pltpu.VMEM((2, 2, 256, 2 * BS), BF16),
            pltpu.VMEM((2, 128, 2 * BS), BF16),
            pltpu.VMEM((NCB * 4, BS), F32),
            pltpu.SemaphoreType.DMA((RANKS,)),
            pltpu.SemaphoreType.DMA((RANKS,)),
            pltpu.SemaphoreType.DMA((RANKS,)),
            pltpu.SemaphoreType.DMA((RANKS,)),
            pltpu.SemaphoreType.DMA((RANKS,)),
        ],
        compiler_params=pltpu.CompilerParams(
            collective_id=0, has_side_effects=True, vmem_limit_bytes=56 << 20
        ),
    )(
        surface_fields[0], cell_area, remap_tiles.reshape(RANKS, SLOTS, BS, BS),
        node_block, pair_blocks, cells, cells, node_block, pair_blocks,
    )
    return out[None]


def solution(mesh):
    return jax.shard_map(
        on_device,
        mesh=mesh,
        in_specs=(
            P("comp", None, "rank"),
            P("comp", "rank"),
            P("rank", None, None),
            P("rank", None),
            P("rank", None, None),
            P("rank", None),
        ),
        out_specs=P("comp", None, "rank"),
        check_vma=False,
    )
```

```python
import jax
import jax.numpy as jnp
from jax import lax
from jax.experimental import pallas as pl
from jax.experimental.pallas import tpu as pltpu
from jax.sharding import PartitionSpec as P

FLUX_IT = 5
MESH = pl.DeviceIdType.MESH
F32 = jnp.float32
BF16 = jnp.bfloat16

RANKS = 64
SLOTS = 8
NCB = 32
BS = 128
F_A = 40
F_F = 20
GROUPS = F_A // 8
CHUNK = 4
NCHUNK = RANKS // CHUNK
ROWS = SLOTS * 8
BACK_ROWS = SLOTS * F_F


def offset(k):
    o = ((k + 1) * 27) & 63
    return o >> 4, (o >> 2) & 3, o & 3


def shifted(home, k, sign):
    dy, dx, dz = offset(k)
    y, x, z = home
    if sign < 0:
        dy, dx, dz = 4 - dy, 4 - dx, 4 - dz
    return (((y + dy) & 3) << 4) + (((x + dx) & 3) << 2) + ((z + dz) & 3)


def kernel(
    fields_hbm, area_hbm, tiles, nblk_hbm, pair_hbm, cell_hbm,
    out,
    tvm, blk, sbuf, rbuf, bsbuf, brbuf, pick, pick2, acc, osurf, wind, wt, stage, stage2, sums2,
    fields, area, nblk, pair, cell, nblk_v, pair_v, cell_v, tsem, ssem, rsem, bssem, brsem, isem,
):
    comp = lax.axis_index("comp")
    rank = lax.axis_index("rank")
    home = (rank >> 4, (rank >> 2) & 3, rank & 3)

    def to_ocean(k):
        return pltpu.make_async_remote_copy(
            src_ref=sbuf.at[k], dst_ref=rbuf.at[k], send_sem=ssem, recv_sem=rsem.at[k],
            device_id=(1, shifted(home, k, 1)), device_id_type=MESH,
        )

    def to_atmosphere(k):
        return pltpu.make_async_remote_copy(
            src_ref=bsbuf.at[k], dst_ref=brbuf.at[k], send_sem=bssem, recv_sem=brsem.at[k],
            device_id=(0, shifted(home, k, -1)), device_id_type=MESH,
        )

    def load_tiles(k):
        return pltpu.make_async_copy(tiles.at[shifted(home, k, 1)], tvm.at[k], tsem.at[k])

    barrier = pltpu.get_barrier_semaphore()

    def greet(k, carry):
        pl.semaphore_signal(
            barrier, inc=1, device_id=(1 - comp, (rank + 42 + jnp.where((k & 1) == 0, k >> 1, -((k + 1) >> 1))) & (RANKS - 1)), device_id_type=MESH
        )
        return carry

    lax.fori_loop(0, RANKS, greet, 0)
    loads = [
        pltpu.make_async_copy(source, target, isem.at[n])
        for n, (source, target) in enumerate(
            (
                (fields_hbm, fields), (nblk_hbm, nblk), (pair_hbm, pair), (cell_hbm, cell),
                (nblk_hbm, nblk_v), (pair_hbm, pair_v), (cell_hbm, cell_v), (area_hbm, area),
            )
        )
    ]
    for load in loads:
        load.start()

    def permuted(b):
        columns = pl.ds(pl.multiple_of(b * BS, BS), BS)
        x = fields[:, columns].astype(F32)
        return [
            x[0:8], x[8:16], jnp.concatenate([x[16:20], x[36:40]], axis=0), x[20:28], x[28:36],
        ]

    @pl.when(comp == 0)
    def _():
        def begin(k, carry):
            load_tiles(k).start()
            return carry

        lax.fori_loop(0, RANKS, begin, 0)
        for load in loads:
            load.wait()

        def arrange(b, carry):
            blk[b] = jnp.concatenate(permuted(b), axis=0).astype(BF16)
            return carry

        lax.fori_loop(0, NCB, arrange, 0)

        def products(k):
            d = shifted(home, k, 1)
            load_tiles(k).wait()
            live = pair[0, d]
            for s in range(0, SLOTS, 2):
                both = []
                for e in (s, s + 1):
                    lhs = blk[nblk[0, d * SLOTS + e]]
                    r = jnp.dot(lhs, tvm[k, e], preferred_element_type=F32)
                    both.append(r * (e < live).astype(F32))
                for g in range(GROUPS):
                    rows = slice(g * 8, g * 8 + 8)
                    sbuf[k, g, s * 8 : s * 8 + 16, :] = jnp.concatenate(
                        [both[0][rows], both[1][rows]], axis=0
                    ).astype(BF16)

        AHEAD = 6
        def ahead(k, carry):
            products(k)
            return carry

        def release(k, carry):
            to_ocean(k).start()
            return carry

        def step(k, carry):
            products(k)
            to_ocean(k).start()
            return carry

        lax.fori_loop(0, AHEAD, ahead, 0)
        pl.semaphore_wait(barrier, RANKS)
        lax.fori_loop(0, AHEAD, release, 0)
        lax.fori_loop(AHEAD, RANKS, step, 0)

        def build(i, carry):
            lane = lax.broadcasted_iota(jnp.int32, (1, 256), 1)
            kk = i * CHUNK + (lane >> 6)
            where_k = shifted(home, kk, 1)
            slot = (lane >> 3) & 7
            q = lax.broadcasted_iota(jnp.int32, (RANKS, 256), 0)
            j = lax.broadcasted_iota(jnp.int32, (RANKS * SLOTS, 256), 0)
            ej = (j == where_k * SLOTS + slot).astype(F32).astype(BF16)
            ed = (q == where_k).astype(F32).astype(BF16)
            nb = jnp.broadcast_to(nblk_v[...].astype(F32), (8, RANKS * SLOTS)).astype(BF16)
            pb = jnp.broadcast_to(pair_v[...].astype(F32), (8, RANKS)).astype(BF16)
            block = jnp.dot(nb, ej, preferred_element_type=F32)[0:1]
            count = jnp.dot(pb, ed, preferred_element_type=F32)[0:1]
            block = jnp.where(slot.astype(F32) < count, block, 100.0)
            key = block * 8.0 + (lane & 7).astype(F32)
            row = lax.broadcasted_iota(jnp.int32, (256, 256), 0).astype(F32)
            pick[i] = (row == key).astype(F32).astype(BF16)
            lane = lax.broadcasted_iota(jnp.int32, (1, 128), 1)
            kk = i * CHUNK + (lane >> 5)
            where_k = shifted(home, kk, 1)
            slot = (lane >> 2) & 7
            q = lax.broadcasted_iota(jnp.int32, (RANKS, 128), 0)
            j = lax.broadcasted_iota(jnp.int32, (RANKS * SLOTS, 128), 0)
            ej = (j == where_k * SLOTS + slot).astype(F32).astype(BF16)
            ed = (q == where_k).astype(F32).astype(BF16)
            block = jnp.dot(nb, ej, preferred_element_type=F32)[0:1]
            count = jnp.dot(pb, ed, preferred_element_type=F32)[0:1]
            block = jnp.where(slot.astype(F32) < count, block, 100.0)
            key = block * 4.0 + (lane & 3).astype(F32)
            row = lax.broadcasted_iota(jnp.int32, (128, 128), 0).astype(F32)
            pick2[i] = (row == key).astype(F32).astype(BF16)
            return carry

        lax.fori_loop(0, NCHUNK, build, 0)
        acc[...] = jnp.zeros_like(acc)
        area[...] = 1.0 / area[...]
        sums2[...] = jnp.zeros_like(sums2)

        def split(r):
            hi = r.astype(BF16)
            return jnp.concatenate([hi, (r - hi.astype(F32)).astype(BF16)], axis=1)

        def collect(i, half):
            for g in (0, 1):
                r = jnp.dot(pick[i], stage[half, g], preferred_element_type=F32)
                acc[g] += r[:, :BS] + r[:, BS:]
            r = jnp.dot(pick2[i], stage2[half], preferred_element_type=F32)
            sums2[...] += r[:, :BS] + r[:, BS:]

        def back_products(i, half):
            for c in range(CHUNK):
                k = i * CHUNK + c
                for p in range(SLOTS // 2):
                    lhs = jnp.concatenate(
                        [
                            brbuf[k, p * 16 : p * 16 + 16],
                            brbuf[k, 64 + p * 16 : 64 + p * 16 + 16],
                            brbuf[k, 128 + p * 8 : 128 + p * 8 + 8],
                        ],
                        axis=0,
                    )
                    rhs = tvm[k, 2 * p : 2 * p + 2].reshape(2 * BS, BS)
                    r = lax.dot_general(
                        lhs, rhs, (((1,), (1,)), ((), ())), preferred_element_type=F32
                    )
                    low, high = r[:, :BS], r[:, BS:]
                    rows = slice(c * 64 + p * 16, c * 64 + p * 16 + 16)
                    stage[half, 0, rows] = split(jnp.concatenate([low[0:8], high[8:16]], axis=0))
                    stage[half, 1, rows] = split(jnp.concatenate([low[16:24], high[24:32]], axis=0))
                    sub = lax.broadcasted_iota(jnp.int32, (8, BS), 0)
                    last = jnp.where(sub < 4, low[32:40], high[32:40])
                    rows = slice(c * 32 + p * 8, c * 32 + p * 8 + 8)
                    stage2[half, rows] = split(last)

        def arrived(i):
            for c in range(CHUNK):
                to_atmosphere(i * CHUNK + c).wait_recv()

        arrived(0)
        pltpu.make_async_copy(sbuf, sbuf, ssem).wait()
        back_products(0, 0)

        def back(m, carry):
            for e in range(2):
                i = 2 * m + 1 + e
                arrived(i)
                collect(i - 1, e)
                back_products(i, 1 - e)
            return carry

        lax.fori_loop(0, (NCHUNK - 2) // 2, back, 0)
        arrived(NCHUNK - 1)
        collect(NCHUNK - 2, 0)
        back_products(NCHUNK - 1, 1)
        collect(NCHUNK - 1, 1)

        for b in range(NCB):
            columns = slice(b * BS, (b + 1) * BS)
            scale = area[0:1, columns]
            out[0:8, 0, columns] = acc[0, b * 8 : b * 8 + 8] * scale
            out[8:16, 0, columns] = acc[1, b * 8 : b * 8 + 8] * scale
            out[16:20, 0, columns] = sums2[b * 4 : b * 4 + 4] * scale

    @pl.when(comp == 1)
    def _():
        for load in loads:
            load.wait()

        def arrange(b, carry):
            rows = pl.ds(pl.multiple_of(b * 8, 8), 8)
            for g, part in enumerate(permuted(b)):
                osurf[g, rows] = part
            return carry

        lax.fori_loop(0, NCB, arrange, 0)

        def build(i, carry):
            lane = lax.broadcasted_iota(jnp.int32, (1, 256), 1)
            kk = i * CHUNK + (lane >> 6)
            where_k = shifted(home, kk, -1)
            slot = (lane >> 3) & 7
            q = lax.broadcasted_iota(jnp.int32, (RANKS, 256), 0)
            ed = (q == where_k).astype(F32).astype(BF16)
            cells = jnp.dot(cell_v[...].astype(F32).astype(BF16), ed, preferred_element_type=F32)
            s = lax.broadcasted_iota(jnp.int32, (SLOTS, 256), 0)
            mine = jnp.sum(jnp.where(s == slot, cells, 0.0), axis=0, keepdims=True)
            key = mine * 8.0 + (lane & 7).astype(F32)
            row = lax.broadcasted_iota(jnp.int32, (256, 256), 0).astype(F32)
            pick[i] = (row == key).astype(F32).astype(BF16)
            return carry

        lax.fori_loop(0, NCHUNK, build, 0)
        acc[...] = jnp.zeros_like(acc)
        pl.semaphore_wait(barrier, RANKS)

        def reduce(i, carry):
            for c in range(CHUNK):
                to_ocean(i * CHUNK + c).wait_recv()
            for groups in ((0, 1), (2, 3), (4,)):
                rhs = [rbuf[pl.ds(i * CHUNK, CHUNK), g].reshape(CHUNK * ROWS, BS) for g in groups]
                r = jnp.dot(pick[i], jnp.concatenate(rhs, axis=1), preferred_element_type=F32)
                for n, g in enumerate(groups):
                    acc[g] += r[:, n * BS : (n + 1) * BS]
            return carry

        lax.fori_loop(0, NCHUNK, reduce, 0)

        def difference(f):
            rows = pl.ds(f, NCB, stride=8)
            return acc[0, rows, :] - osurf[0, rows, :]

        wind_u = difference(0)
        wind_v = difference(1)
        wind_speed = jnp.sqrt(wind_u * wind_u + wind_v * wind_v + 0.25)
        stability = 1.0 + 4.0 * jax.nn.sigmoid(difference(2))
        transfer = jnp.ones_like(wind_speed)
        for sweep in range(FLUX_IT):
            transfer = 1.0 / (1.0 + stability * transfer)
        wind[...] = transfer * wind_speed

        for c in range(NCB):
            rows = slice(c * 8, c * 8 + 8)
            columns = slice(c * BS, (c + 1) * BS)
            scale = jnp.broadcast_to(wind[c : c + 1], (8, BS))
            a = jnp.broadcast_to(area[0:1, columns], (8, BS))
            x = [acc[g, rows] for g in range(GROUPS)]
            o = [osurf[g, rows] for g in range(GROUPS)]
            first = scale * (x[0] - o[0]) + x[3] * o[3]
            second = scale * (x[1] - o[1]) + x[4] * o[4]
            third = scale * (x[2] - o[2]) + pltpu.roll(x[2] * o[2], 4, 0)
            out[0:8, 0, columns] = first
            out[8:16, 0, columns] = second
            out[16:20, 0, columns] = third[0:4]
            sub = lax.broadcasted_iota(jnp.int32, (8, BS), 0)
            third = jnp.where(sub < 4, third * a, 0.0).astype(BF16).astype(F32)
            wt[c, 0] = (first * a).astype(BF16).astype(F32)
            wt[c, 1] = (second * a).astype(BF16).astype(F32)
            wt[c, 2] = third
            wt[c, 3] = pltpu.roll(third, 4, 0)

        def send_back(k, carry):
            q = shifted(home, k, -1)
            cells = [cell[s, q] for s in range(SLOTS)]
            for g in (0, 1):
                for s in range(0, SLOTS, 2):
                    bsbuf[k, g * 64 + s * 8 : g * 64 + s * 8 + 16] = jnp.concatenate(
                        [wt[cells[s], g], wt[cells[s + 1], g]], axis=0
                    ).astype(BF16)
            for s in range(0, SLOTS, 4):
                bsbuf[k, 128 + s * 4 : 128 + s * 4 + 16] = jnp.concatenate(
                    [
                        wt[cells[s], 2] + wt[cells[s + 1], 3],
                        wt[cells[s + 2], 2] + wt[cells[s + 3], 3],
                    ],
                    axis=0,
                ).astype(BF16)
            to_atmosphere(k).start()
            return carry

        lax.fori_loop(0, RANKS, send_back, 0)

        pltpu.make_async_copy(bsbuf, bsbuf, bssem).wait()


def on_device(surface_fields, cell_area, remap_tiles, pair_blocks, slot_cell, node_block):
    vmem = pl.BlockSpec(memory_space=pltpu.VMEM)
    hbm = pl.BlockSpec(memory_space=pl.ANY)
    out = pl.pallas_call(
        kernel,
        out_shape=jax.ShapeDtypeStruct((F_F, 1, NCB * BS), F32),
        in_specs=[hbm] * 6,
        out_specs=vmem,
        scratch_shapes=[
            pltpu.VMEM((RANKS, SLOTS, BS, BS), BF16),
            pltpu.VMEM((NCB, F_A, BS), BF16),
            pltpu.VMEM((RANKS, GROUPS, ROWS, BS), BF16),
            pltpu.VMEM((RANKS, GROUPS, ROWS, BS), BF16),
            pltpu.VMEM((RANKS, BACK_ROWS, BS), BF16),
            pltpu.VMEM((RANKS, BACK_ROWS, BS), BF16),
            pltpu.VMEM((NCHUNK, 256, 256), BF16),
            pltpu.VMEM((NCHUNK, 128, 128), BF16),
            pltpu.VMEM((GROUPS, NCB * 8, BS), F32),
            pltpu.VMEM((GROUPS, NCB * 8, BS), F32),
            pltpu.VMEM((NCB, BS), F32),
            pltpu.VMEM((NCB, 4, 8, BS), F32),
            pltpu.VMEM((2, 2, 256, 2 * BS), BF16),
            pltpu.VMEM((2, 128, 2 * BS), BF16),
            pltpu.VMEM((NCB * 4, BS), F32),
            pltpu.VMEM((F_A, NCB * BS), BF16),
            pltpu.VMEM((1, NCB * BS), F32),
            pltpu.SMEM((1, RANKS * SLOTS), jnp.int32),
            pltpu.SMEM((1, RANKS), jnp.int32),
            pltpu.SMEM((SLOTS, RANKS), jnp.int32),
            pltpu.VMEM((1, RANKS * SLOTS), jnp.int32),
            pltpu.VMEM((1, RANKS), jnp.int32),
            pltpu.VMEM((SLOTS, RANKS), jnp.int32),
            pltpu.SemaphoreType.DMA((RANKS,)),
            pltpu.SemaphoreType.DMA,
            pltpu.SemaphoreType.DMA((RANKS,)),
            pltpu.SemaphoreType.DMA,
            pltpu.SemaphoreType.DMA((RANKS,)),
            pltpu.SemaphoreType.DMA((8,)),
        ],
        compiler_params=pltpu.CompilerParams(
            collective_id=0, has_side_effects=True, vmem_limit_bytes=56 << 20
        ),
    )(
        surface_fields[0], cell_area, remap_tiles.reshape(RANKS, SLOTS, BS, BS),
        node_block, pair_blocks, slot_cell[0].T,
    )
    return out.transpose(1, 0, 2)


def solution(mesh):
    return jax.shard_map(
        on_device,
        mesh=mesh,
        in_specs=(
            P("comp", None, "rank"),
            P("comp", "rank"),
            P("rank", None, None),
            P("rank", None),
            P("rank", None, None),
            P("rank", None),
        ),
        out_specs=P("comp", None, "rank"),
        check_vma=False,
    )
```

```python
import jax
import jax.numpy as jnp
from jax import lax
from jax.experimental import pallas as pl
from jax.experimental.pallas import tpu as pltpu
from jax.sharding import PartitionSpec as P

FLUX_IT = 5
MESH = pl.DeviceIdType.MESH
F32 = jnp.float32
BF16 = jnp.bfloat16

RANKS = 64
SLOTS = 8
NCB = 32
BS = 128
F_A = 40
F_F = 20
GROUPS = F_A // 8
CHUNK = 4
NCHUNK = RANKS // CHUNK
ROWS = SLOTS * 8
BACK_ROWS = SLOTS * F_F


def offset(k):
    k = k + 1
    o = (k * 27) & 63
    return (o >> 2) & 3, o >> 4, o & 3


def shifted(home, k, sign):
    dy, dx, dz = offset(k)
    y, x, z = home
    if sign < 0:
        dy, dx, dz = 4 - dy, 4 - dx, 4 - dz
    return (((y + dy) & 3) << 4) + (((x + dx) & 3) << 2) + ((z + dz) & 3)


def kernel(
    fields_hbm, area_hbm, tiles, nblk_hbm, pair_hbm, cell_hbm,
    out,
    tvm, blk, sbuf, rbuf, bsbuf, brbuf, pick, pick2, acc, osurf, wind, wt, stage, stage2, sums2,
    fields, area, nblk, pair, cell, nblk_v, pair_v, cell_v, tsem, ssem, rsem, bssem, brsem, isem,
):
    comp = lax.axis_index("comp")
    rank = lax.axis_index("rank")
    home = (rank >> 4, (rank >> 2) & 3, rank & 3)

    def to_ocean(k):
        return pltpu.make_async_remote_copy(
            src_ref=sbuf.at[k], dst_ref=rbuf.at[k], send_sem=ssem, recv_sem=rsem.at[k],
            device_id=(1, shifted(home, k, 1)), device_id_type=MESH,
        )

    def to_atmosphere(k):
        return pltpu.make_async_remote_copy(
            src_ref=bsbuf.at[k], dst_ref=brbuf.at[k], send_sem=bssem, recv_sem=brsem.at[k],
            device_id=(0, shifted(home, k, -1)), device_id_type=MESH,
        )

    def load_tiles(k):
        return pltpu.make_async_copy(tiles.at[shifted(home, k, 1)], tvm.at[k], tsem.at[k])

    barrier = pltpu.get_barrier_semaphore()

    def greet(k, carry):
        pl.semaphore_signal(
            barrier, inc=1, device_id=(1 - comp, (rank + 42 + jnp.where((k & 1) == 0, k >> 1, -((k + 1) >> 1))) & (RANKS - 1)), device_id_type=MESH
        )
        return carry

    lax.fori_loop(0, RANKS, greet, 0)
    loads = [
        pltpu.make_async_copy(source, target, isem.at[n])
        for n, (source, target) in enumerate(
            (
                (fields_hbm, fields), (nblk_hbm, nblk), (pair_hbm, pair), (cell_hbm, cell),
                (nblk_hbm, nblk_v), (pair_hbm, pair_v), (cell_hbm, cell_v), (area_hbm, area),
            )
        )
    ]
    for load in loads:
        load.start()

    def permuted(b):
        columns = pl.ds(pl.multiple_of(b * BS, BS), BS)
        x = fields[:, columns].astype(F32)
        return [
            x[0:8], x[8:16], jnp.concatenate([x[16:20], x[36:40]], axis=0), x[20:28], x[28:36],
        ]

    @pl.when(comp == 0)
    def _():
        def begin(k, carry):
            load_tiles(k).start()
            return carry

        lax.fori_loop(0, RANKS, begin, 0)
        for load in loads:
            load.wait()

        def arrange(b, carry):
            blk[b] = jnp.concatenate(permuted(b), axis=0).astype(BF16)
            return carry

        lax.fori_loop(0, NCB, arrange, 0)

        def products(k):
            d = shifted(home, k, 1)
            load_tiles(k).wait()
            live = pair[0, d]
            for s in range(0, SLOTS, 2):
                both = []
                for e in (s, s + 1):
                    lhs = blk[nblk[0, d * SLOTS + e]]
                    r = jnp.dot(lhs, tvm[k, e], preferred_element_type=F32)
                    both.append(r * (e < live).astype(F32))
                for g in range(GROUPS):
                    rows = slice(g * 8, g * 8 + 8)
                    sbuf[k, g, s * 8 : s * 8 + 16, :] = jnp.concatenate(
                        [both[0][rows], both[1][rows]], axis=0
                    ).astype(BF16)

        AHEAD = 6
        def ahead(k, carry):
            products(k)
            return carry

        def release(k, carry):
            to_ocean(k).start()
            return carry

        def step(m, carry):
            for e in range(2):
                products(AHEAD + 2 * m + e)
            for e in range(2):
                to_ocean(AHEAD + 2 * m + e).start()
            return carry

        lax.fori_loop(0, AHEAD, ahead, 0)
        pl.semaphore_wait(barrier, RANKS)
        lax.fori_loop(0, AHEAD, release, 0)
        lax.fori_loop(0, (RANKS - AHEAD) // 2, step, 0)

        def build(i, carry):
            lane = lax.broadcasted_iota(jnp.int32, (1, 256), 1)
            kk = i * CHUNK + (lane >> 6)
            where_k = shifted(home, kk, 1)
            slot = (lane >> 3) & 7
            q = lax.broadcasted_iota(jnp.int32, (RANKS, 256), 0)
            j = lax.broadcasted_iota(jnp.int32, (RANKS * SLOTS, 256), 0)
            ej = (j == where_k * SLOTS + slot).astype(F32).astype(BF16)
            ed = (q == where_k).astype(F32).astype(BF16)
            nb = jnp.broadcast_to(nblk_v[...].astype(F32), (8, RANKS * SLOTS)).astype(BF16)
            pb = jnp.broadcast_to(pair_v[...].astype(F32), (8, RANKS)).astype(BF16)
            block = jnp.dot(nb, ej, preferred_element_type=F32)[0:1]
            count = jnp.dot(pb, ed, preferred_element_type=F32)[0:1]
            block = jnp.where(slot.astype(F32) < count, block, 100.0)
            key = block * 8.0 + (lane & 7).astype(F32)
            row = lax.broadcasted_iota(jnp.int32, (256, 256), 0).astype(F32)
            pick[i] = (row == key).astype(F32).astype(BF16)
            lane = lax.broadcasted_iota(jnp.int32, (1, 128), 1)
            kk = i * CHUNK + (lane >> 5)
            where_k = shifted(home, kk, 1)
            slot = (lane >> 2) & 7
            q = lax.broadcasted_iota(jnp.int32, (RANKS, 128), 0)
            j = lax.broadcasted_iota(jnp.int32, (RANKS * SLOTS, 128), 0)
            ej = (j == where_k * SLOTS + slot).astype(F32).astype(BF16)
            ed = (q == where_k).astype(F32).astype(BF16)
            block = jnp.dot(nb, ej, preferred_element_type=F32)[0:1]
            count = jnp.dot(pb, ed, preferred_element_type=F32)[0:1]
            block = jnp.where(slot.astype(F32) < count, block, 100.0)
            key = block * 4.0 + (lane & 3).astype(F32)
            row = lax.broadcasted_iota(jnp.int32, (128, 128), 0).astype(F32)
            pick2[i] = (row == key).astype(F32).astype(BF16)
            return carry

        lax.fori_loop(0, NCHUNK, build, 0)
        acc[...] = jnp.zeros_like(acc)
        area[...] = 1.0 / area[...]
        sums2[...] = jnp.zeros_like(sums2)

        def split(r):
            hi = r.astype(BF16)
            return jnp.concatenate([hi, (r - hi.astype(F32)).astype(BF16)], axis=1)

        def collect(i, half):
            for g in (0, 1):
                r = jnp.dot(pick[i], stage[half, g], preferred_element_type=F32)
                acc[g] += r[:, :BS] + r[:, BS:]
            r = jnp.dot(pick2[i], stage2[half], preferred_element_type=F32)
            sums2[...] += r[:, :BS] + r[:, BS:]

        def back_products(i, half):
            for c in range(CHUNK):
                k = i * CHUNK + c
                for p in range(SLOTS // 2):
                    lhs = jnp.concatenate(
                        [
                            brbuf[k, p * 16 : p * 16 + 16],
                            brbuf[k, 64 + p * 16 : 64 + p * 16 + 16],
                            brbuf[k, 128 + p * 8 : 128 + p * 8 + 8],
                        ],
                        axis=0,
                    )
                    rhs = tvm[k, 2 * p : 2 * p + 2].reshape(2 * BS, BS)
                    r = lax.dot_general(
                        lhs, rhs, (((1,), (1,)), ((), ())), preferred_element_type=F32
                    )
                    low, high = r[:, :BS], r[:, BS:]
                    rows = slice(c * 64 + p * 16, c * 64 + p * 16 + 16)
                    stage[half, 0, rows] = split(jnp.concatenate([low[0:8], high[8:16]], axis=0))
                    stage[half, 1, rows] = split(jnp.concatenate([low[16:24], high[24:32]], axis=0))
                    sub = lax.broadcasted_iota(jnp.int32, (8, BS), 0)
                    last = jnp.where(sub < 4, low[32:40], high[32:40])
                    rows = slice(c * 32 + p * 8, c * 32 + p * 8 + 8)
                    stage2[half, rows] = split(last)

        def arrived(i):
            for c in range(CHUNK):
                to_atmosphere(i * CHUNK + c).wait_recv()

        arrived(0)
        pltpu.make_async_copy(sbuf, sbuf, ssem).wait()
        back_products(0, 0)

        def back(m, carry):
            for e in range(2):
                i = 2 * m + 1 + e
                arrived(i)
                collect(i - 1, e)
                back_products(i, 1 - e)
            return carry

        lax.fori_loop(0, (NCHUNK - 2) // 2, back, 0)
        arrived(NCHUNK - 1)
        collect(NCHUNK - 2, 0)
        back_products(NCHUNK - 1, 1)
        collect(NCHUNK - 1, 1)

        for b in range(NCB):
            columns = slice(b * BS, (b + 1) * BS)
            scale = area[0:1, columns]
            out[0:8, 0, columns] = acc[0, b * 8 : b * 8 + 8] * scale
            out[8:16, 0, columns] = acc[1, b * 8 : b * 8 + 8] * scale
            out[16:20, 0, columns] = sums2[b * 4 : b * 4 + 4] * scale

    @pl.when(comp == 1)
    def _():
        for load in loads:
            load.wait()

        def arrange(b, carry):
            rows = pl.ds(pl.multiple_of(b * 8, 8), 8)
            for g, part in enumerate(permuted(b)):
                osurf[g, rows] = part
            return carry

        lax.fori_loop(0, NCB, arrange, 0)

        def build(i, carry):
            lane = lax.broadcasted_iota(jnp.int32, (1, 256), 1)
            kk = i * CHUNK + (lane >> 6)
            where_k = shifted(home, kk, -1)
            slot = (lane >> 3) & 7
            q = lax.broadcasted_iota(jnp.int32, (RANKS, 256), 0)
            ed = (q == where_k).astype(F32).astype(BF16)
            cells = jnp.dot(cell_v[...].astype(F32).astype(BF16), ed, preferred_element_type=F32)
            s = lax.broadcasted_iota(jnp.int32, (SLOTS, 256), 0)
            mine = jnp.sum(jnp.where(s == slot, cells, 0.0), axis=0, keepdims=True)
            key = mine * 8.0 + (lane & 7).astype(F32)
            row = lax.broadcasted_iota(jnp.int32, (256, 256), 0).astype(F32)
            pick[i] = (row == key).astype(F32).astype(BF16)
            return carry

        lax.fori_loop(0, NCHUNK, build, 0)
        acc[...] = jnp.zeros_like(acc)
        pl.semaphore_wait(barrier, RANKS)

        def reduce(i, carry):
            for c in range(CHUNK):
                to_ocean(i * CHUNK + c).wait_recv()
            for groups in ((0, 1), (2, 3), (4,)):
                rhs = [rbuf[pl.ds(i * CHUNK, CHUNK), g].reshape(CHUNK * ROWS, BS) for g in groups]
                r = jnp.dot(pick[i], jnp.concatenate(rhs, axis=1), preferred_element_type=F32)
                for n, g in enumerate(groups):
                    acc[g] += r[:, n * BS : (n + 1) * BS]
            return carry

        lax.fori_loop(0, NCHUNK, reduce, 0)

        def difference(f):
            rows = pl.ds(f, NCB, stride=8)
            return acc[0, rows, :] - osurf[0, rows, :]

        wind_u = difference(0)
        wind_v = difference(1)
        wind_speed = jnp.sqrt(wind_u * wind_u + wind_v * wind_v + 0.25)
        stability = 1.0 + 4.0 * jax.nn.sigmoid(difference(2))
        transfer = jnp.ones_like(wind_speed)
        for sweep in range(FLUX_IT):
            transfer = 1.0 / (1.0 + stability * transfer)
        wind[...] = transfer * wind_speed

        for c in range(NCB):
            rows = slice(c * 8, c * 8 + 8)
            columns = slice(c * BS, (c + 1) * BS)
            scale = jnp.broadcast_to(wind[c : c + 1], (8, BS))
            a = jnp.broadcast_to(area[0:1, columns], (8, BS))
            x = [acc[g, rows] for g in range(GROUPS)]
            o = [osurf[g, rows] for g in range(GROUPS)]
            first = scale * (x[0] - o[0]) + x[3] * o[3]
            second = scale * (x[1] - o[1]) + x[4] * o[4]
            third = scale * (x[2] - o[2]) + pltpu.roll(x[2] * o[2], 4, 0)
            out[0:8, 0, columns] = first
            out[8:16, 0, columns] = second
            out[16:20, 0, columns] = third[0:4]
            sub = lax.broadcasted_iota(jnp.int32, (8, BS), 0)
            third = jnp.where(sub < 4, third * a, 0.0).astype(BF16).astype(F32)
            wt[c, 0] = (first * a).astype(BF16).astype(F32)
            wt[c, 1] = (second * a).astype(BF16).astype(F32)
            wt[c, 2] = third
            wt[c, 3] = pltpu.roll(third, 4, 0)

        def send_back(k, carry):
            q = shifted(home, k, -1)
            cells = [cell[s, q] for s in range(SLOTS)]
            for g in (0, 1):
                for s in range(0, SLOTS, 2):
                    bsbuf[k, g * 64 + s * 8 : g * 64 + s * 8 + 16] = jnp.concatenate(
                        [wt[cells[s], g], wt[cells[s + 1], g]], axis=0
                    ).astype(BF16)
            for s in range(0, SLOTS, 4):
                bsbuf[k, 128 + s * 4 : 128 + s * 4 + 16] = jnp.concatenate(
                    [
                        wt[cells[s], 2] + wt[cells[s + 1], 3],
                        wt[cells[s + 2], 2] + wt[cells[s + 3], 3],
                    ],
                    axis=0,
                ).astype(BF16)
            to_atmosphere(k).start()
            return carry

        lax.fori_loop(0, RANKS, send_back, 0)

        pltpu.make_async_copy(bsbuf, bsbuf, bssem).wait()


def on_device(surface_fields, cell_area, remap_tiles, pair_blocks, slot_cell, node_block):
    vmem = pl.BlockSpec(memory_space=pltpu.VMEM)
    hbm = pl.BlockSpec(memory_space=pl.ANY)
    out = pl.pallas_call(
        kernel,
        out_shape=jax.ShapeDtypeStruct((F_F, 1, NCB * BS), F32),
        in_specs=[hbm] * 6,
        out_specs=vmem,
        scratch_shapes=[
            pltpu.VMEM((RANKS, SLOTS, BS, BS), BF16),
            pltpu.VMEM((NCB, F_A, BS), BF16),
            pltpu.VMEM((RANKS, GROUPS, ROWS, BS), BF16),
            pltpu.VMEM((RANKS, GROUPS, ROWS, BS), BF16),
            pltpu.VMEM((RANKS, BACK_ROWS, BS), BF16),
            pltpu.VMEM((RANKS, BACK_ROWS, BS), BF16),
            pltpu.VMEM((NCHUNK, 256, 256), BF16),
            pltpu.VMEM((NCHUNK, 128, 128), BF16),
            pltpu.VMEM((GROUPS, NCB * 8, BS), F32),
            pltpu.VMEM((GROUPS, NCB * 8, BS), F32),
            pltpu.VMEM((NCB, BS), F32),
            pltpu.VMEM((NCB, 4, 8, BS), F32),
            pltpu.VMEM((2, 2, 256, 2 * BS), BF16),
            pltpu.VMEM((2, 128, 2 * BS), BF16),
            pltpu.VMEM((NCB * 4, BS), F32),
            pltpu.VMEM((F_A, NCB * BS), BF16),
            pltpu.VMEM((1, NCB * BS), F32),
            pltpu.SMEM((1, RANKS * SLOTS), jnp.int32),
            pltpu.SMEM((1, RANKS), jnp.int32),
            pltpu.SMEM((SLOTS, RANKS), jnp.int32),
            pltpu.VMEM((1, RANKS * SLOTS), jnp.int32),
            pltpu.VMEM((1, RANKS), jnp.int32),
            pltpu.VMEM((SLOTS, RANKS), jnp.int32),
            pltpu.SemaphoreType.DMA((RANKS,)),
            pltpu.SemaphoreType.DMA,
            pltpu.SemaphoreType.DMA((RANKS,)),
            pltpu.SemaphoreType.DMA,
            pltpu.SemaphoreType.DMA((RANKS,)),
            pltpu.SemaphoreType.DMA((8,)),
        ],
        compiler_params=pltpu.CompilerParams(
            collective_id=0, has_side_effects=True, vmem_limit_bytes=56 << 20
        ),
    )(
        surface_fields[0], cell_area, remap_tiles.reshape(RANKS, SLOTS, BS, BS),
        node_block, pair_blocks, slot_cell[0].T,
    )
    return out.transpose(1, 0, 2)


def solution(mesh):
    return jax.shard_map(
        on_device,
        mesh=mesh,
        in_specs=(
            P("comp", None, "rank"),
            P("comp", "rank"),
            P("rank", None, None),
            P("rank", None),
            P("rank", None, None),
            P("rank", None),
        ),
        out_specs=P("comp", None, "rank"),
        check_vma=False,
    )
```

```python
import jax
import jax.numpy as jnp
from jax import lax
from jax.experimental import pallas as pl
from jax.experimental.pallas import tpu as pltpu
from jax.sharding import PartitionSpec as P

FLUX_IT = 5
MESH = pl.DeviceIdType.MESH
F32 = jnp.float32
BF16 = jnp.bfloat16

RANKS = 64
SLOTS = 8
NCB = 32
BS = 128
F_A = 40
F_F = 20
GROUPS = F_A // 8
CHUNK = 4
NCHUNK = RANKS // CHUNK
ROWS = SLOTS * 8
BACK_ROWS = SLOTS * F_F


def offset(k):
    k = k + 1
    o = (k * 27) & 63
    return (o >> 2) & 3, o >> 4, o & 3


def shifted(home, k, sign):
    dy, dx, dz = offset(k)
    y, x, z = home
    if sign < 0:
        dy, dx, dz = 4 - dy, 4 - dx, 4 - dz
    return (((y + dy) & 3) << 4) + (((x + dx) & 3) << 2) + ((z + dz) & 3)


def kernel(
    fields_hbm, area_hbm, tiles, nblk_hbm, pair_hbm, cell_hbm,
    out,
    tvm, blk, sbuf, rbuf, bsbuf, brbuf, pick, pick2, acc, osurf, wind, wt, stage, stage2, sums2,
    fields, area, nblk, pair, cell, nblk_v, pair_v, cell_v, tsem, ssem, rsem, bssem, brsem, isem,
):
    comp = lax.axis_index("comp")
    rank = lax.axis_index("rank")
    home = (rank >> 4, (rank >> 2) & 3, rank & 3)

    def to_ocean(k):
        return pltpu.make_async_remote_copy(
            src_ref=sbuf.at[k], dst_ref=rbuf.at[k], send_sem=ssem, recv_sem=rsem.at[k],
            device_id=(1, shifted(home, k, 1)), device_id_type=MESH,
        )

    def to_atmosphere(k):
        return pltpu.make_async_remote_copy(
            src_ref=bsbuf.at[k], dst_ref=brbuf.at[k], send_sem=bssem, recv_sem=brsem.at[k],
            device_id=(0, shifted(home, k, -1)), device_id_type=MESH,
        )

    def load_tiles(k):
        return pltpu.make_async_copy(tiles.at[shifted(home, k, 1)], tvm.at[k], tsem.at[k])

    barrier = pltpu.get_barrier_semaphore()

    def greet(k, carry):
        pl.semaphore_signal(
            barrier, inc=1, device_id=(1 - comp, (rank + 42 + jnp.where((k & 1) == 0, k >> 1, -((k + 1) >> 1))) & (RANKS - 1)), device_id_type=MESH
        )
        return carry

    lax.fori_loop(0, RANKS, greet, 0, unroll=8)
    loads = [
        pltpu.make_async_copy(source, target, isem.at[n])
        for n, (source, target) in enumerate(
            (
                (fields_hbm, fields), (nblk_hbm, nblk), (pair_hbm, pair), (cell_hbm, cell),
                (nblk_hbm, nblk_v), (pair_hbm, pair_v), (cell_hbm, cell_v), (area_hbm, area),
            )
        )
    ]
    for load in loads:
        load.start()

    def permuted(b):
        columns = pl.ds(pl.multiple_of(b * BS, BS), BS)
        x = fields[:, columns].astype(F32)
        return [
            x[0:8], x[8:16], jnp.concatenate([x[16:20], x[36:40]], axis=0), x[20:28], x[28:36],
        ]

    @pl.when(comp == 0)
    def _():
        def begin(k, carry):
            load_tiles(k).start()
            return carry

        lax.fori_loop(0, RANKS, begin, 0, unroll=8)
        for load in loads:
            load.wait()

        def arrange(b, carry):
            blk[b] = jnp.concatenate(permuted(b), axis=0).astype(BF16)
            return carry

        lax.fori_loop(0, NCB, arrange, 0)

        def products(k):
            d = shifted(home, k, 1)
            load_tiles(k).wait()
            live = pair[0, d]
            for s in range(0, SLOTS, 2):
                both = []
                for e in (s, s + 1):
                    lhs = blk[nblk[0, d * SLOTS + e]]
                    r = jnp.dot(lhs, tvm[k, e], preferred_element_type=F32)
                    both.append(r * (e < live).astype(F32))
                for g in range(GROUPS):
                    rows = slice(g * 8, g * 8 + 8)
                    sbuf[k, g, s * 8 : s * 8 + 16, :] = jnp.concatenate(
                        [both[0][rows], both[1][rows]], axis=0
                    ).astype(BF16)

        AHEAD = 6
        def ahead(k, carry):
            products(k)
            return carry

        def release(k, carry):
            to_ocean(k).start()
            return carry

        def step(m, carry):
            for e in range(2):
                products(AHEAD + 2 * m + e)
            for e in range(2):
                to_ocean(AHEAD + 2 * m + e).start()
            return carry

        lax.fori_loop(0, AHEAD, ahead, 0)
        pl.semaphore_wait(barrier, RANKS)
        lax.fori_loop(0, AHEAD, release, 0)
        lax.fori_loop(0, (RANKS - AHEAD) // 2, step, 0)

        def build(i, carry):
            lane = lax.broadcasted_iota(jnp.int32, (1, 256), 1)
            kk = i * CHUNK + (lane >> 6)
            where_k = shifted(home, kk, 1)
            slot = (lane >> 3) & 7
            q = lax.broadcasted_iota(jnp.int32, (RANKS, 256), 0)
            j = lax.broadcasted_iota(jnp.int32, (RANKS * SLOTS, 256), 0)
            ej = (j == where_k * SLOTS + slot).astype(F32).astype(BF16)
            ed = (q == where_k).astype(F32).astype(BF16)
            nb = jnp.broadcast_to(nblk_v[...].astype(F32), (8, RANKS * SLOTS)).astype(BF16)
            pb = jnp.broadcast_to(pair_v[...].astype(F32), (8, RANKS)).astype(BF16)
            block = jnp.dot(nb, ej, preferred_element_type=F32)[0:1]
            count = jnp.dot(pb, ed, preferred_element_type=F32)[0:1]
            block = jnp.where(slot.astype(F32) < count, block, 100.0)
            key = block * 8.0 + (lane & 7).astype(F32)
            row = lax.broadcasted_iota(jnp.int32, (256, 256), 0).astype(F32)
            pick[i] = (row == key).astype(F32).astype(BF16)
            lane = lax.broadcasted_iota(jnp.int32, (1, 128), 1)
            kk = i * CHUNK + (lane >> 5)
            where_k = shifted(home, kk, 1)
            slot = (lane >> 2) & 7
            q = lax.broadcasted_iota(jnp.int32, (RANKS, 128), 0)
            j = lax.broadcasted_iota(jnp.int32, (RANKS * SLOTS, 128), 0)
            ej = (j == where_k * SLOTS + slot).astype(F32).astype(BF16)
            ed = (q == where_k).astype(F32).astype(BF16)
            block = jnp.dot(nb, ej, preferred_element_type=F32)[0:1]
            count = jnp.dot(pb, ed, preferred_element_type=F32)[0:1]
            block = jnp.where(slot.astype(F32) < count, block, 100.0)
            key = block * 4.0 + (lane & 3).astype(F32)
            row = lax.broadcasted_iota(jnp.int32, (128, 128), 0).astype(F32)
            pick2[i] = (row == key).astype(F32).astype(BF16)
            return carry

        lax.fori_loop(0, NCHUNK, build, 0)
        acc[...] = jnp.zeros_like(acc)
        area[...] = 1.0 / area[...]
        sums2[...] = jnp.zeros_like(sums2)

        def split(r):
            hi = r.astype(BF16)
            return jnp.concatenate([hi, (r - hi.astype(F32)).astype(BF16)], axis=1)

        def collect(i, half):
            for g in (0, 1):
                r = jnp.dot(pick[i], stage[half, g], preferred_element_type=F32)
                acc[g] += r[:, :BS] + r[:, BS:]
            r = jnp.dot(pick2[i], stage2[half], preferred_element_type=F32)
            sums2[...] += r[:, :BS] + r[:, BS:]

        def back_products(i, half):
            for c in range(CHUNK):
                k = i * CHUNK + c
                for p in range(SLOTS // 2):
                    lhs = jnp.concatenate(
                        [
                            brbuf[k, p * 16 : p * 16 + 16],
                            brbuf[k, 64 + p * 16 : 64 + p * 16 + 16],
                            brbuf[k, 128 + p * 8 : 128 + p * 8 + 8],
                        ],
                        axis=0,
                    )
                    rhs = tvm[k, 2 * p : 2 * p + 2].reshape(2 * BS, BS)
                    r = lax.dot_general(
                        lhs, rhs, (((1,), (1,)), ((), ())), preferred_element_type=F32
                    )
                    low, high = r[:, :BS], r[:, BS:]
                    rows = slice(c * 64 + p * 16, c * 64 + p * 16 + 16)
                    stage[half, 0, rows] = split(jnp.concatenate([low[0:8], high[8:16]], axis=0))
                    stage[half, 1, rows] = split(jnp.concatenate([low[16:24], high[24:32]], axis=0))
                    sub = lax.broadcasted_iota(jnp.int32, (8, BS), 0)
                    last = jnp.where(sub < 4, low[32:40], high[32:40])
                    rows = slice(c * 32 + p * 8, c * 32 + p * 8 + 8)
                    stage2[half, rows] = split(last)

        def arrived(i):
            for c in range(CHUNK):
                to_atmosphere(i * CHUNK + c).wait_recv()

        arrived(0)
        pltpu.make_async_copy(sbuf, sbuf, ssem).wait()
        back_products(0, 0)

        def back(m, carry):
            for e in range(2):
                i = 2 * m + 1 + e
                arrived(i)
                collect(i - 1, e)
                back_products(i, 1 - e)
            return carry

        lax.fori_loop(0, (NCHUNK - 2) // 2, back, 0)
        arrived(NCHUNK - 1)
        collect(NCHUNK - 2, 0)
        back_products(NCHUNK - 1, 1)
        collect(NCHUNK - 1, 1)

        for b in range(NCB):
            columns = slice(b * BS, (b + 1) * BS)
            scale = area[0:1, columns]
            out[0:8, 0, columns] = acc[0, b * 8 : b * 8 + 8] * scale
            out[8:16, 0, columns] = acc[1, b * 8 : b * 8 + 8] * scale
            out[16:20, 0, columns] = sums2[b * 4 : b * 4 + 4] * scale

    @pl.when(comp == 1)
    def _():
        for load in loads:
            load.wait()

        def arrange(b, carry):
            rows = pl.ds(pl.multiple_of(b * 8, 8), 8)
            for g, part in enumerate(permuted(b)):
                osurf[g, rows] = part
            return carry

        lax.fori_loop(0, NCB, arrange, 0)

        def build(i, carry):
            lane = lax.broadcasted_iota(jnp.int32, (1, 256), 1)
            kk = i * CHUNK + (lane >> 6)
            where_k = shifted(home, kk, -1)
            slot = (lane >> 3) & 7
            q = lax.broadcasted_iota(jnp.int32, (RANKS, 256), 0)
            ed = (q == where_k).astype(F32).astype(BF16)
            cells = jnp.dot(cell_v[...].astype(F32).astype(BF16), ed, preferred_element_type=F32)
            s = lax.broadcasted_iota(jnp.int32, (SLOTS, 256), 0)
            mine = jnp.sum(jnp.where(s == slot, cells, 0.0), axis=0, keepdims=True)
            key = mine * 8.0 + (lane & 7).astype(F32)
            row = lax.broadcasted_iota(jnp.int32, (256, 256), 0).astype(F32)
            pick[i] = (row == key).astype(F32).astype(BF16)
            return carry

        lax.fori_loop(0, NCHUNK, build, 0)
        acc[...] = jnp.zeros_like(acc)
        pl.semaphore_wait(barrier, RANKS)

        def reduce(i, carry):
            for c in range(CHUNK):
                to_ocean(i * CHUNK + c).wait_recv()
            for groups in ((0, 1), (2, 3), (4,)):
                rhs = [rbuf[pl.ds(i * CHUNK, CHUNK), g].reshape(CHUNK * ROWS, BS) for g in groups]
                r = jnp.dot(pick[i], jnp.concatenate(rhs, axis=1), preferred_element_type=F32)
                for n, g in enumerate(groups):
                    acc[g] += r[:, n * BS : (n + 1) * BS]
            return carry

        lax.fori_loop(0, NCHUNK, reduce, 0)

        def difference(f):
            rows = pl.ds(f, NCB, stride=8)
            return acc[0, rows, :] - osurf[0, rows, :]

        wind_u = difference(0)
        wind_v = difference(1)
        wind_speed = jnp.sqrt(wind_u * wind_u + wind_v * wind_v + 0.25)
        stability = 1.0 + 4.0 * jax.nn.sigmoid(difference(2))
        transfer = jnp.ones_like(wind_speed)
        for sweep in range(FLUX_IT):
            transfer = 1.0 / (1.0 + stability * transfer)
        wind[...] = transfer * wind_speed

        for c in range(NCB):
            rows = slice(c * 8, c * 8 + 8)
            columns = slice(c * BS, (c + 1) * BS)
            scale = jnp.broadcast_to(wind[c : c + 1], (8, BS))
            a = jnp.broadcast_to(area[0:1, columns], (8, BS))
            x = [acc[g, rows] for g in range(GROUPS)]
            o = [osurf[g, rows] for g in range(GROUPS)]
            first = scale * (x[0] - o[0]) + x[3] * o[3]
            second = scale * (x[1] - o[1]) + x[4] * o[4]
            third = scale * (x[2] - o[2]) + pltpu.roll(x[2] * o[2], 4, 0)
            out[0:8, 0, columns] = first
            out[8:16, 0, columns] = second
            out[16:20, 0, columns] = third[0:4]
            sub = lax.broadcasted_iota(jnp.int32, (8, BS), 0)
            third = jnp.where(sub < 4, third * a, 0.0).astype(BF16).astype(F32)
            wt[c, 0] = (first * a).astype(BF16).astype(F32)
            wt[c, 1] = (second * a).astype(BF16).astype(F32)
            wt[c, 2] = third
            wt[c, 3] = pltpu.roll(third, 4, 0)

        def send_back(k, carry):
            q = shifted(home, k, -1)
            cells = [cell[s, q] for s in range(SLOTS)]
            for g in (0, 1):
                for s in range(0, SLOTS, 2):
                    bsbuf[k, g * 64 + s * 8 : g * 64 + s * 8 + 16] = jnp.concatenate(
                        [wt[cells[s], g], wt[cells[s + 1], g]], axis=0
                    ).astype(BF16)
            for s in range(0, SLOTS, 4):
                bsbuf[k, 128 + s * 4 : 128 + s * 4 + 16] = jnp.concatenate(
                    [
                        wt[cells[s], 2] + wt[cells[s + 1], 3],
                        wt[cells[s + 2], 2] + wt[cells[s + 3], 3],
                    ],
                    axis=0,
                ).astype(BF16)
            to_atmosphere(k).start()
            return carry

        lax.fori_loop(0, RANKS, send_back, 0, unroll=2)

        pltpu.make_async_copy(bsbuf, bsbuf, bssem).wait()


def on_device(surface_fields, cell_area, remap_tiles, pair_blocks, slot_cell, node_block):
    vmem = pl.BlockSpec(memory_space=pltpu.VMEM)
    hbm = pl.BlockSpec(memory_space=pl.ANY)
    out = pl.pallas_call(
        kernel,
        out_shape=jax.ShapeDtypeStruct((F_F, 1, NCB * BS), F32),
        in_specs=[hbm] * 6,
        out_specs=vmem,
        scratch_shapes=[
            pltpu.VMEM((RANKS, SLOTS, BS, BS), BF16),
            pltpu.VMEM((NCB, F_A, BS), BF16),
            pltpu.VMEM((RANKS, GROUPS, ROWS, BS), BF16),
            pltpu.VMEM((RANKS, GROUPS, ROWS, BS), BF16),
            pltpu.VMEM((RANKS, BACK_ROWS, BS), BF16),
            pltpu.VMEM((RANKS, BACK_ROWS, BS), BF16),
            pltpu.VMEM((NCHUNK, 256, 256), BF16),
            pltpu.VMEM((NCHUNK, 128, 128), BF16),
            pltpu.VMEM((GROUPS, NCB * 8, BS), F32),
            pltpu.VMEM((GROUPS, NCB * 8, BS), F32),
            pltpu.VMEM((NCB, BS), F32),
            pltpu.VMEM((NCB, 4, 8, BS), F32),
            pltpu.VMEM((2, 2, 256, 2 * BS), BF16),
            pltpu.VMEM((2, 128, 2 * BS), BF16),
            pltpu.VMEM((NCB * 4, BS), F32),
            pltpu.VMEM((F_A, NCB * BS), BF16),
            pltpu.VMEM((1, NCB * BS), F32),
            pltpu.SMEM((1, RANKS * SLOTS), jnp.int32),
            pltpu.SMEM((1, RANKS), jnp.int32),
            pltpu.SMEM((SLOTS, RANKS), jnp.int32),
            pltpu.VMEM((1, RANKS * SLOTS), jnp.int32),
            pltpu.VMEM((1, RANKS), jnp.int32),
            pltpu.VMEM((SLOTS, RANKS), jnp.int32),
            pltpu.SemaphoreType.DMA((RANKS,)),
            pltpu.SemaphoreType.DMA,
            pltpu.SemaphoreType.DMA((RANKS,)),
            pltpu.SemaphoreType.DMA,
            pltpu.SemaphoreType.DMA((RANKS,)),
            pltpu.SemaphoreType.DMA((8,)),
        ],
        compiler_params=pltpu.CompilerParams(
            collective_id=0, has_side_effects=True, vmem_limit_bytes=56 << 20
        ),
    )(
        surface_fields[0], cell_area, remap_tiles.reshape(RANKS, SLOTS, BS, BS),
        node_block, pair_blocks, slot_cell[0].T,
    )
    return out.transpose(1, 0, 2)


def solution(mesh):
    return jax.shard_map(
        on_device,
        mesh=mesh,
        in_specs=(
            P("comp", None, "rank"),
            P("comp", "rank"),
            P("rank", None, None),
            P("rank", None),
            P("rank", None, None),
            P("rank", None),
        ),
        out_specs=P("comp", None, "rank"),
        check_vma=False,
    )
```
